512 devices in a mesh: row: 16 (over y, x), col: 32 (over z, core).
Axes of the slice: x: 4, y: 4, z: 16, core: 2. Of those that a mesh axis runs over, the one named last changes fastest.
Arguments:
- residual_in: float32 [8, 16, 128, 256], P(None, 'row', None, 'col'), may hold values from -6 to 6
- diag_inverse: bfloat16 [8, 16, 256, 256], P(None, 'row'), may hold values from -0.04 to 1.04, as said below
- lower_blocks: bfloat16 [7, 16, 3, 256, 256], P(None, 'row'), may hold values from -0.15625 to 0.15625
- column_lists: int32 [7, 16, 3], replicated, may hold values from 0 to 111, as said below
Outputs:
- precond: float32 [8, 16, 128, 256], P(None, 'row', None, 'col')
The draws below stay inside these ranges and needn't reach their ends.
Inputs may be any that keep to these rules, and one draw needn't show every extreme that they name: `column_lists`: for a block row of level s, every entry names a block row of a level below s; its first entry names a block row of level s - 1, and every block row of level s - 1 is named so by exactly one block row of level s. `diag_inverse`: each block is the identity plus small entries.
All inputs are finite; a program needn't handle non-finite values.
Results may differ from the reference program's by a relative error of at most 0.0003.
Values sent between devices are 32-bit elements; how exact they have to be, the bound alone decides.
A program may use at most 64 MiB of HBM per device.

```python
import jax
import jax.numpy as jnp
from jax import lax

BS = 256
KB = 3
SLOTS = 8
OWNERS = 16
PROBES = 128


def draw_column_lists(key, part):
    shifts = jax.random.randint(jax.random.fold_in(key, 11), (SLOTS - 1, 1), 0, OWNERS)
    owner_ids = jnp.arange(OWNERS, dtype=jnp.int32)[None, :]
    levels = jnp.arange(1, SLOTS, dtype=jnp.int32)[:, None]
    leading = (levels - 1) * OWNERS + (owner_ids + shifts) % OWNERS
    limits = jnp.broadcast_to((levels * OWNERS)[:, :, None], (SLOTS - 1, OWNERS, KB - 1))
    others = jax.random.randint(jax.random.fold_in(key, 12), (SLOTS - 1, OWNERS, KB - 1), 0, limits)
    return jnp.concatenate([leading[:, :, None], others], axis=2).astype(jnp.int32)


def draw_diag_inverse(key, part):
    identity = (jnp.arange(BS)[:, None] == jnp.arange(BS)[None, :]).astype(jnp.float32)
    shape = (SLOTS, OWNERS, BS, BS)
    noise = jax.random.uniform(key, shape, jnp.float32, -0.03, 0.03)
    return (identity + noise).astype(jnp.bfloat16)


def shard_levels(key, dims, pieces, least, largest):
    loudness = 1.0
    for dim, shards_of in pieces:
        heights = jax.random.uniform(jax.random.fold_in(jax.random.fold_in(key, 6), dim), (shards_of,), jnp.float32, least / len(pieces), largest / len(pieces))
        loudness = loudness * jnp.repeat(jnp.exp(heights), dims[dim] // shards_of).reshape((-1,) + (1,) * (len(dims) - 1 - dim))
    return loudness


def scatter_about(own_key, dims, spread, limit, cuts=(), kind=jnp.bfloat16):
    result = jax.random.normal(own_key, dims, jnp.float32) * spread
    if len(cuts) > 0:
        result = shard_levels(own_key, dims, cuts, -0.22, 0.18) * result
    return jnp.clip(result, min=-limit, max=limit).astype(kind)


def setup_inputs(seed: int = 0) -> dict:
    keys = jax.random.split(jax.random.key(seed), 5)
    return {
        "residual_in": scatter_about(keys[0], (SLOTS, OWNERS, PROBES, BS), 1.0, 6.0, ((1, 16), (3, 32)), jnp.float32),
        "diag_inverse": draw_diag_inverse(jax.random.fold_in(keys[4], 71), 0),
        "lower_blocks": scatter_about(keys[2], (SLOTS - 1, OWNERS, KB, BS, BS), (6 * BS) ** -0.5, 0.15625, ((1, 16),)),
        "column_lists": draw_column_lists(jax.random.fold_in(keys[4], 71), 0),
    }


def reference(residual_in, diag_inverse, lower_blocks, column_lists):
    highest = lax.Precision.HIGHEST
    inverses = diag_inverse.astype(jnp.float32)
    lowers = lower_blocks.astype(jnp.float32)
    total_blocks = SLOTS * OWNERS
    forward = jnp.zeros((total_blocks, PROBES, BS), jnp.float32)
    for current in range(SLOTS):
        source = residual_in[current]
        if current > 0:
            pulled = forward[column_lists[current - 1]]
            source = source - jnp.einsum("rkpc,rkdc->rpd", pulled, lowers[current - 1], precision=highest)
        solved = jnp.einsum("rpc,rdc->rpd", source, inverses[current], precision=highest)
        forward = forward.at[current * OWNERS:(current + 1) * OWNERS].set(solved)
    accumulated = jnp.zeros((total_blocks, PROBES, BS), jnp.float32)
    backward = jnp.zeros((total_blocks, PROBES, BS), jnp.float32)
    for current in reversed(range(SLOTS)):
        lower_end = current * OWNERS
        upper_end = (current + 1) * OWNERS
        source = forward[lower_end:upper_end] - accumulated[lower_end:upper_end]
        solved = jnp.einsum("rpc,rcd->rpd", source, inverses[current], precision=highest)
        backward = backward.at[lower_end:upper_end].set(solved)
        if current > 0:
            contributions = jnp.einsum("rpd,rkdc->rkpc", solved, lowers[current - 1], precision=highest)
            targets = column_lists[current - 1].reshape(-1).astype(jnp.int32)
            accumulated = accumulated.at[targets].add(contributions.reshape(-1, PROBES, BS))
    return backward.reshape(SLOTS, OWNERS, PROBES, BS)
```

```python
import functools

import jax
import jax.numpy as jnp
from jax import lax
from jax.experimental import pallas as pl
from jax.experimental.pallas import tpu as pltpu
from jax.sharding import PartitionSpec as P

MESH = pl.DeviceIdType.MESH
NT = (((1,), (1,)), ((), ()))
NN = (((1,), (0,)), ((), ()))


def split(packed):
    first = lax.broadcasted_iota(jnp.int32, packed.shape, 0) < 4
    wide = jnp.concatenate([jnp.where(first, packed, 0.0), jnp.where(first, 0.0, packed)], axis=1)
    high = wide.astype(jnp.bfloat16).astype(jnp.float32)
    return jnp.concatenate([high, wide - high], axis=0).astype(jnp.bfloat16)


def merge(product):
    both = product[:8] + product[8:]
    left, right = both[:, :128], both[:, 128:]
    left = left + pltpu.roll(left, 4, 0)
    right = right + pltpu.roll(right, 4, 0)
    first = lax.broadcasted_iota(jnp.int32, left.shape, 0) < 4
    return jnp.where(first, left, right)


def times(rows, block, dims):
    return lax.dot_general(rows, block, dims, preferred_element_type=jnp.float32)


def kernel(levels, n, own_ref, r_ref, d_ref, l_ref, out_ref, mine, came, done, part, base, give, back,
           fsend, frecv, bsend, brecv):
    me = lax.axis_index("row")
    peers = [lax.rem(me + j, n) for j in range(1, n)]
    barrier = pltpu.get_barrier_semaphore()
    for peer in peers:
        pl.semaphore_signal(barrier, inc=1, device_id={"row": peer}, device_id_type=MESH)
    pl.semaphore_wait(barrier, n - 1)

    mine[0] = merge(times(split(r_ref[0]), d_ref[0], NT))

    def forward(level, carry):
        last = level - 1
        for j, peer in enumerate(peers):
            pltpu.make_async_remote_copy(
                mine.at[last], came.at[last, j], fsend.at[last], frecv.at[last],
                device_id={"row": peer}, device_id_type=MESH).start()
        done[last * n + me] = mine[last]
        pltpu.make_async_copy(came.at[last], came.at[last], frecv.at[last]).wait()
        for j in range(1, n):
            done[last * n + lax.rem(me - j + n, n)] = came[last, j - 1]
        total = None
        for k in range(3):
            term = times(split(done[own_ref[last, k]]), l_ref[last, k], NT)
            total = term if total is None else total + term
        mine[level] = merge(times(split(r_ref[level] - merge(total)), d_ref[level], NT))
        return carry

    lax.fori_loop(1, levels, forward, 0)
    top = levels - 1
    out_ref[top] = merge(times(split(mine[top]), d_ref[top], NN))
    base[...] = jnp.zeros_like(base)

    def backward(step, carry):
        level = top - step
        low = level - 1
        rows = split(out_ref[level])
        news = [merge(times(rows, l_ref[low, k], NN)) for k in range(3)]
        for k in range(3):
            part[low, k] = news[k]
        wants = [jnp.full((8, 128), own_ref[low, k] - low * n, jnp.int32) for k in range(3)]
        for r in range(n):
            message = base[r]
            for k in range(3):
                message = message + jnp.where(wants[k] == r, news[k], 0.0)
            give[low, r] = message
        for j, peer in enumerate(peers):
            pltpu.make_async_remote_copy(
                give.at[low, peer], back.at[low, j], bsend.at[low], brecv.at[low],
                device_id={"row": peer}, device_id_type=MESH).start()
        own = give[low, me]

        base[...] = jnp.zeros_like(base)

        def older(source, carry):
            for k in range(1, 3):
                want = jnp.full((8, 128), own_ref[source, k] - (low - 1) * n, jnp.int32)
                value = part[source, k]
                for r in range(n):
                    base[r] = base[r] + jnp.where(want == r, value, 0.0)
            return carry

        lax.fori_loop(low, top, older, 0)
        pltpu.make_async_copy(back.at[low], back.at[low], brecv.at[low]).wait()
        for j in range(n - 1):
            own = own + back[low, j]
        out_ref[low] = merge(times(split(mine[low] - own), d_ref[low], NN))
        return carry

    lax.fori_loop(0, top, backward, 0)

    def drain(level, carry):
        pltpu.make_async_copy(came.at[level], came.at[level], fsend.at[level]).wait()
        pltpu.make_async_copy(back.at[level], back.at[level], bsend.at[level]).wait()
        return carry

    lax.fori_loop(0, top, drain, 0)


def shards(residual_in, diag_inverse, lower_blocks, column_lists):
    sweep_input = lax.all_to_all(residual_in, "col", split_axis=2, concat_axis=3, tiled=True)[:, 0]
    levels, probes, cells = sweep_input.shape
    n = lax.axis_size("row")
    packed = sweep_input.reshape(levels, probes, 2, 128).transpose(0, 2, 1, 3).reshape(levels, 8, 128)
    own = lax.dynamic_index_in_dim(column_lists, lax.axis_index("row"), 1, keepdims=False)
    vmem = pl.BlockSpec(memory_space=pltpu.VMEM)
    f32 = jnp.float32
    solved = pl.pallas_call(
        functools.partial(kernel, levels, n),
        out_shape=jax.ShapeDtypeStruct((levels, 8, 128), f32),
        in_specs=[pl.BlockSpec(memory_space=pltpu.SMEM), vmem, vmem, vmem],
        out_specs=vmem,
        scratch_shapes=[
            pltpu.VMEM((levels, 8, 128), f32),
            pltpu.VMEM((levels - 1, n - 1, 8, 128), f32),
            pltpu.VMEM(((levels - 1) * n, 8, 128), f32),
            pltpu.VMEM((levels - 1, 3, 8, 128), f32),
            pltpu.VMEM((n, 8, 128), f32),
            pltpu.VMEM((levels - 1, n, 8, 128), f32),
            pltpu.VMEM((levels - 1, n - 1, 8, 128), f32),
            pltpu.SemaphoreType.DMA((levels - 1,)),
            pltpu.SemaphoreType.DMA((levels - 1,)),
            pltpu.SemaphoreType.DMA((levels - 1,)),
            pltpu.SemaphoreType.DMA((levels - 1,)),
        ],
        compiler_params=pltpu.CompilerParams(
            collective_id=0, has_side_effects=True, vmem_limit_bytes=32 * 1024 * 1024),
    )(own, packed, diag_inverse[:, 0], lower_blocks[:, 0])
    backward = solved.reshape(levels, 2, probes, 128).transpose(0, 2, 1, 3).reshape(levels, probes, cells)
    return lax.all_to_all(backward[:, None], "col", split_axis=3, concat_axis=2, tiled=True)


def solution(mesh):
    placed = (
        P(None, "row", None, "col"),
        P(None, "row", None, None),
        P(None, "row", None, None, None),
        P(),
    )
    return jax.shard_map(
        shards, mesh=mesh, in_specs=placed, out_specs=P(None, "row", None, "col"), check_vma=False
    )
```
